32 devices in a mesh: groups: 1, expert: 32 (over z, y, x, core).
Axes of the slice: x: 2, y: 2, z: 4, core: 2. Of those that a mesh axis runs over, the one named last changes fastest.
Arguments:
- normed: bfloat16 [256, 7168], P(('groups', 'expert')), may hold values from -6 to 6
- expert_ids: int32 [256, 2], P(('groups', 'expert')), may hold values from 0 to 3, all different within a row; in each aligned block of 8 rows (0 to 7, 8 to 15, ...) at most 5 rows name the same one
- gate_levels: int32 [256, 2], P(('groups', 'expert')), may hold values from 1 to 255
- placement: int32 [32], replicated, may hold values from 0 to 3, as said below
- w_gate: bfloat16 [32, 7168, 256], P('expert'), may hold values from -0.0625 to 0.0625
- w_up: bfloat16 [32, 7168, 256], P('expert'), may hold values from -0.0625 to 0.0625
- w_down: bfloat16 [32, 256, 7168], P('expert'), may hold values from -0.125 to 0.125
- q_latent: bfloat16 [256, 64, 512], P(('groups', 'expert')), may hold values from -48 to 48
- q_rope: bfloat16 [256, 4096], P(('groups', 'expert')), may hold values from -48 to 48
- cache_latent: bfloat16 [256, 64, 512], P(('groups', 'expert')), may hold values from -6 to 6
- cache_rope: bfloat16 [256, 64, 64], P(('groups', 'expert')), may hold values from -6 to 6
- lengths: int32 [256], P(('groups', 'expert')), may hold values from 2 to 64, as said below
Outputs:
- moe_out: bfloat16 [256, 7168], P(('groups', 'expert'))
- attended: bfloat16 [256, 64, 512], P(('groups', 'expert'))
The draws below stay inside these ranges and needn't reach their ends.
Inputs may be any that keep to these rules, and one draw needn't show every extreme that they name: `expert_ids`: within the rows of one device an expert is named at most 5 times. `placement`: each expert is held by exactly 8 devices. `lengths`: some device holds a request of 64 positions.
All inputs are finite; a program needn't handle non-finite values.
Results may differ from the reference program's by a relative error of at most 0.0085.
Values may be sent and summed in bfloat16 or wider, within the bound.
A program may use at most 128 MiB of HBM per device.

```python
import math
import jax
import jax.numpy as jnp
import numpy as np
from jax import lax

D = 7168
FF = 2048
FF_DEV = 256
TOPK = 2
HEADS = 64
LAT = 512
ROPE = 64
ROWS = 8
LMAX = 64
SPLIT = 8
SLICES = 32
EXPERTS = 4
CAP = 5
TOKENS = 256


def attention_draw(key):
    key_lat, key_rope, key_query, key_qrope = jax.random.split(jax.random.fold_in(key, 11), 4)
    cache_lat = jnp.clip(jax.random.normal(key_lat, (TOKENS, LMAX, LAT), jnp.float32), -6.0, 6.0)
    cache_pos = jnp.clip(jax.random.normal(key_rope, (TOKENS, ROPE, LMAX), jnp.float32), -6.0, 6.0)
    query_lat = jnp.clip(jax.random.normal(key_query, (TOKENS, HEADS, LAT), jnp.float32), -6.0, 6.0)
    query_pos = jnp.clip(jax.random.normal(key_qrope, (TOKENS, HEADS, ROPE), jnp.float32), -6.0, 6.0)
    return (query_lat, query_pos.reshape(TOKENS, HEADS * ROPE), cache_lat, cache_pos)


def draw_q_latent(key, part):
    return attention_draw(key)[0].astype(jnp.bfloat16)


def draw_q_rope(key, part):
    return attention_draw(key)[1].astype(jnp.bfloat16)


def draw_cache_latent(key, part):
    return attention_draw(key)[2].astype(jnp.bfloat16)


def draw_cache_rope(key, part):
    return attention_draw(key)[3].astype(jnp.bfloat16)


def draw_placement(key, part):
    order = jax.random.permutation(jax.random.fold_in(key, 5), SLICES)
    return (order // SPLIT).astype(jnp.int32)


def draw_lengths(key, part):
    key_cap, key_long, key_len, key_pick = jax.random.split(jax.random.fold_in(key, 3), 4)
    devices = TOKENS // ROWS
    device_caps = jax.random.randint(key_cap, (devices,), LMAX // 4, LMAX + 1)
    longest = jax.random.randint(key_long, (), 0, devices)
    device_caps = jnp.where(jnp.arange(devices) == longest, LMAX, device_caps)
    drawn_lengths = jax.random.randint(key_len, (devices, ROWS), 2, device_caps[:, None] + 1)
    chosen = jax.random.randint(key_pick, (devices,), 0, ROWS)
    drawn_lengths = jnp.where(jnp.arange(ROWS)[None, :] == chosen[:, None], device_caps[:, None], drawn_lengths)
    return drawn_lengths.reshape(TOKENS).astype(jnp.int32)


def with_ends(values, key, smallest, high):
    extent = values.shape
    spot = [jax.random.randint(jax.random.fold_in(key, axis), (), 0, extent[axis]) for axis in range(len(extent))]
    values = values.at[tuple(spot)].set(smallest)
    longest = extent.index(max(extent))
    spot[longest] = (spot[longest] + 1) % extent[longest]
    return values.at[tuple(spot)].set(high)


def block_levels(key, shape, cuts, low, largest):
    gain, own = 1.0, jax.random.fold_in(key, 6)
    for dim, parts in cuts:
        heights = jnp.exp(jax.random.uniform(jax.random.fold_in(own, dim), (parts,), jnp.float32, low / len(cuts), largest / len(cuts)))
        gain = gain * jnp.repeat(heights, shape[dim] // parts).reshape([-1 if axis == dim else 1 for axis in range(len(shape))])
    return gain


def routed_block(stream_key, own, number, rows, count, top, bound, slope):
    order = jax.random.permutation(stream_key, count)
    packed, usual = load_shares(count, rows * top, bound, slope, True), load_shares(count, rows * top, bound, slope, False)
    places = jnp.arange(count)

    def named(sizes, rotation):
        used = int((sizes > 0).sum())
        fixed = max(1, used // 4)
        shifted = fixed + (places - fixed + rotation * (used - fixed)) % max(1, count - fixed)
        return jnp.zeros((count,), jnp.int32).at[order[jnp.where(places < fixed, places, shifted)]].set(jnp.asarray(sizes, jnp.int32))

    sizes = jnp.where(number % 4 == 0, named(packed, number // 4), named(usual, number - number // 4 - 1))
    mixed = jax.random.permutation(jax.random.fold_in(own, 3), count)
    source_of, taker = mixed[0:count // 2 * 2:2], mixed[1:count // 2 * 2:2]
    slack = jnp.minimum(sizes[source_of] - 1, bound - sizes[taker]) // 2
    slack = jnp.where((source_of == order[0]) | (taker == order[0]) | (sizes[taker] == 0), 0, jnp.maximum(slack, 0))
    shifted = jax.random.randint(jax.random.fold_in(own, 4), (count // 2,), 0, 1 << 20) % (slack + 1)
    sizes = sizes.at[source_of].add(-shifted).at[taker].add(shifted)
    members = jnp.searchsorted(jnp.cumsum(sizes), jnp.arange(rows * top), side="right").astype(jnp.int32)
    grid = members.reshape(top, rows).T
    grid = grid[jax.random.permutation(jax.random.fold_in(own, 1), rows)]
    rotation = jax.random.randint(jax.random.fold_in(own, 2), (rows, 1), 0, top)
    return jnp.take_along_axis(grid, (jnp.arange(top)[None, :] + rotation) % top, axis=1)


def load_shares(amount, total, reach, lean, full):
    weights = [(1 << 20) // math.isqrt(rank ** lean) + 1 for rank in range(1, amount + 1)]
    largest = reach if full else min(reach, max(-(-total // amount), total * weights[0] // sum(weights)))
    least = 1 if total - largest >= amount - 1 else 0
    given, rest = [largest] + [least] * (amount - 1), total - largest - least * (amount - 1)
    while rest > 0:
        movable = [i for i in range(1, amount) if given[i] < largest] or [i for i in range(1, amount) if given[i] < reach]
        whole, remaining = sum([weights[i] for i in movable]), rest
        for i in movable:
            addition = min(reach - given[i], max(1, remaining * weights[i] // whole), rest)
            given[i] = given[i] + addition
            rest = rest - addition
    return np.array(given)


def noise(own_key, extent, scale, most, cuts=(), dtype=jnp.bfloat16):
    entries = scale * jax.random.normal(own_key, extent, jnp.float32)
    if cuts:
        entries = entries * block_levels(own_key, extent, cuts, -0.22, 0.18)
    return jnp.clip(entries, -most, most).astype(dtype)


def setup_inputs(seed: int = 0, part: int = 0) -> dict:
    key_list = jax.random.split(jax.random.key(seed), 13)
    part_keys = jax.random.split(jax.random.fold_in(key_list[12], part), 13)
    normed = noise(part_keys[0], (TOKENS, D), 1.0, 6.0, ((0, 32),))
    expert_ids_keys = jax.random.split(jax.random.fold_in(part_keys[1], 1), TOKENS // ROWS)
    expert_ids_turns = jax.random.permutation(jax.random.fold_in(part_keys[1], 3), TOKENS // ROWS)
    expert_ids = jax.vmap(lambda own, number: routed_block(jax.random.fold_in(part_keys[1], 2), own, number, ROWS, EXPERTS, TOPK, CAP, 2))(expert_ids_keys, expert_ids_turns).reshape((TOKENS, TOPK))
    gate_levels = with_ends(jax.random.randint(part_keys[2], (TOKENS, TOPK), 1, 256), jax.random.fold_in(part_keys[2], 1), 1, 255).astype(jnp.int32)
    placement = draw_placement(jax.random.fold_in(key_list[12], 71), part)
    w_gate = noise(key_list[4], (SLICES, D, FF_DEV), D ** -0.5, 0.0625, ((0, 32),))
    w_up = noise(key_list[5], (SLICES, D, FF_DEV), D ** -0.5, 0.0625, ((0, 32),))
    w_down = noise(key_list[6], (SLICES, FF_DEV, D), FF ** -0.5, 0.125, ((0, 32),))
    q_latent = draw_q_latent(jax.random.fold_in(jax.random.fold_in(key_list[12], part), 71), part)
    q_rope = draw_q_rope(jax.random.fold_in(jax.random.fold_in(key_list[12], part), 71), part)
    cache_latent = draw_cache_latent(jax.random.fold_in(jax.random.fold_in(key_list[12], part), 71), part)
    cache_rope = draw_cache_rope(jax.random.fold_in(jax.random.fold_in(key_list[12], part), 71), part)
    lengths = draw_lengths(jax.random.fold_in(jax.random.fold_in(key_list[12], part), 71), part)
    return dict(normed=normed, expert_ids=expert_ids, gate_levels=gate_levels, placement=placement, w_gate=w_gate, w_up=w_up, w_down=w_down, q_latent=q_latent, q_rope=q_rope, cache_latent=cache_latent, cache_rope=cache_rope, lengths=lengths)


score_scale = 192.0 ** -0.5
route_scale = 2.5


def route_weights(gate_levels):
    levels = gate_levels.astype(jnp.float32)
    return route_scale * levels / jnp.sum(levels, axis=1, keepdims=True)


def reference(normed, expert_ids, gate_levels, placement, w_gate, w_up, w_down, q_latent, q_rope, cache_latent, cache_rope, lengths):
    weights = route_weights(gate_levels)

    def one_slice(running, inputs):
        gate_mat, up_mat, down_mat, expert = inputs
        gate_proj = jnp.dot(normed, gate_mat, preferred_element_type=jnp.float32)
        up_proj = jnp.dot(normed, up_mat, preferred_element_type=jnp.float32)
        hidden = (jax.nn.silu(gate_proj) * up_proj).astype(jnp.bfloat16)
        partial_value = jnp.dot(hidden, down_mat, preferred_element_type=jnp.float32).astype(jnp.bfloat16)
        partial_value = lax.optimization_barrier(partial_value).astype(jnp.float32)
        coefficient = jnp.sum(jnp.where(expert_ids == expert, weights, jnp.zeros_like(weights)), axis=1)
        return running + coefficient[:, None] * partial_value, None

    running, ignored = lax.scan(one_slice, jnp.zeros((TOKENS, D), jnp.float32), (w_gate, w_up, w_down, placement))
    moe_out = running.astype(jnp.bfloat16)

    rope_query = q_rope.reshape(TOKENS, HEADS, ROPE).astype(jnp.float32)
    scores = jnp.einsum('bhc,blc->bhl', q_latent.astype(jnp.float32), cache_latent.astype(jnp.float32))
    scores = scores + jnp.einsum('bhr,brl->bhl', rope_query, cache_rope.astype(jnp.float32))
    scores = scores * score_scale
    visible = jnp.arange(LMAX)[None, None, :] < lengths[:, None, None]
    scores = jnp.where(visible, scores, jnp.full_like(scores, -1e30))
    top_score = jnp.max(scores, axis=-1, keepdims=True)
    exponent = jnp.where(visible, jnp.exp(scores - top_score), jnp.zeros_like(scores))
    probs = (exponent / jnp.sum(exponent, axis=-1, keepdims=True)).astype(jnp.bfloat16)
    attended = jnp.einsum('bhl,blc->bhc', probs.astype(jnp.float32), cache_latent.astype(jnp.float32)).astype(jnp.bfloat16)
    return (moe_out, attended)
```

```python
import functools

import jax
import jax.numpy as jnp
from jax import lax
from jax.experimental import pallas as pl
from jax.experimental.pallas import tpu as pltpu
from jax.sharding import PartitionSpec as P

score_scale = 192.0 ** (-0.5)
route_scale = 2.5
BF, F32 = jnp.bfloat16, jnp.float32
EXTRA = 128
UP, DOWN, SIDE_A, SIDE_B, CORE = range(5)


def chip_grid(n):
    return (4, 2, 2) if n == 32 else (n // 2, 1, 1)


def body(
    n,
    normed_ref, ids_ref, lev_ref, len_ref, place_ref, wg_hbm, wu_hbm, wd_hbm,
    ql_ref, qr_ref, cl_ref, cr_ref,
    moe_ref, att_ref,
    xs, acc, rc, rb, ra, ru, rd, wg, wu, wd, h3, cf, rq, gacc, uacc,
    w_sem, ag_ss, ag_rs, rs_ss, rc_s, rb_s, ra_s, ru_s, rd_s,
):
    Z, Y, X = chip_grid(n)
    plane = Y * X
    planar = plane > 1
    chips = n // 2
    R, D = normed_ref.shape
    F = wg.shape[1]
    top = ids_ref.shape[1]
    me = lax.axis_index("expert")
    c = me % 2
    chip = me // 2
    z = chip // plane
    y = (chip % plane) // X
    x = chip % X
    a = x * (1 - c) + y * c
    b = y * (1 - c) + x * c
    sa = (1 - c) + X * c
    sb = X * (1 - c) + c
    peer_a = me + 2 * (1 - 2 * a) * sa
    peer_b = me + 2 * (1 - 2 * b) * sb
    peer_c = 2 * chip + 1 - c
    up, down = me + 2 * plane, me - 2 * plane

    def at(zz, aa, bb):
        if planar:
            return zz * plane + aa * sa + bb * sb
        return zz

    for src, dst, s in ((wg_hbm, wg, 0), (wu_hbm, wu, 1), (wd_hbm, wd, 2)):
        pltpu.make_async_copy(src.at[0], dst, w_sem.at[s]).start()

    xs[chip, c, :, pl.ds(0, D)] = normed_ref[...]
    lane = lax.broadcasted_iota(jnp.int32, (R, EXTRA), 1)
    tail = jnp.zeros((R, EXTRA), F32)
    for k in range(top):
        tail = jnp.where(lane == k, ids_ref[:, k : k + 1].astype(F32), tail)
        tail = jnp.where(lane == top + k, lev_ref[:, k : k + 1].astype(F32), tail)
    xs[chip, c, :, pl.ds(D, EXTRA)] = tail.astype(BF)

    barrier = pltpu.get_barrier_semaphore()

    def greet(dev):
        pl.semaphore_signal(barrier, inc=1, device_id={"expert": dev})

    greet(peer_c)
    if planar:
        greet(peer_a)
        greet(peer_b)
    pl.when(z < Z - 1)(lambda: greet(up))
    pl.when(z > 0)(lambda: greet(down))
    ends = jnp.where(z == 0, 1, 0) + jnp.where(z == Z - 1, 1, 0)
    pl.semaphore_wait(barrier, (5 if planar else 3) - ends)

    def ag(i, cc, way, dev):
        return pltpu.make_async_remote_copy(
            xs.at[i, cc], xs.at[i, cc], ag_ss.at[way, i], ag_rs.at[i, cc], device_id={"expert": dev}
        )

    def got(i, cc):
        ag(i, cc, CORE, peer_c).wait_recv()

    def share(i):
        if planar:
            ag(i, c, SIDE_A, peer_a).start()
            ag(i, c, SIDE_B, peer_b).start()
        ag(i, c, CORE, peer_c).start()

    pl.when(z < Z - 1)(lambda: ag(chip, c, UP, up).start())
    pl.when(z > 0)(lambda: ag(chip, c, DOWN, down).start())
    share(chip)

    qr = qr_ref[...].astype(F32)
    heads, rope = ql_ref.shape[1], cr_ref.shape[1]
    for h in range(heads):
        rq[h * R : (h + 1) * R, :rope] = qr[:, h * rope : (h + 1) * rope]

    lmax = cl_ref.shape[1]

    def attend(t):
        keys = cl_ref[t]
        rope_q = rq[pl.ds(t, heads, stride=R), :rope].astype(BF)
        s = lax.dot_general(ql_ref[t], keys, (((1,), (1,)), ((), ())), preferred_element_type=F32)
        s = s + jnp.dot(rope_q, cr_ref[t], preferred_element_type=F32)
        s = s * score_scale
        seen = lax.broadcasted_iota(jnp.int32, (heads, lmax), 1) < len_ref[t]
        s = jnp.where(seen, s, -1e30)
        e = jnp.where(seen, jnp.exp(s - jnp.max(s, axis=-1, keepdims=True)), 0.0)
        p = (e / jnp.sum(e, axis=-1, keepdims=True)).astype(BF)
        att_ref[t] = jnp.dot(p, keys, preferred_element_type=F32).astype(BF)

    def from_a(zz):
        i = at(zz, 1 - a, b)
        got(i, c)
        ag(i, c, SIDE_B, peer_b).start()
        ag(i, c, CORE, peer_c).start()

    if planar:
        from_a(z)

    def z_step(d, carry):
        @pl.when(z - d >= 0)
        def _():
            i = at(z - d, a, b)
            got(i, c)
            pl.when(z < Z - 1)(lambda: ag(i, c, UP, up).start())
            share(i)

        @pl.when(z + d < Z)
        def _():
            i = at(z + d, a, b)
            got(i, c)
            pl.when(z > 0)(lambda: ag(i, c, DOWN, down).start())
            share(i)

        if planar:
            pl.when(z - d >= 0)(lambda: from_a(z - d))
            pl.when(z + d < Z)(lambda: from_a(z + d))
        return carry

    lax.fori_loop(1, Z, z_step, 0)

    if planar:
        def from_b(k, carry):
            attend(k)
            i = at(k // 2, k % 2, 1 - b)
            got(i, c)
            ag(i, c, CORE, peer_c).start()
            return carry

        lax.fori_loop(0, 2 * Z, from_b, 0)
        first = min(2 * Z, R)
    else:
        first = 0
    for t in range(first, R):
        attend(t)

    def from_core(i, carry):
        got(i, 1 - c)
        return carry

    lax.fori_loop(0, chips, from_core, 0)

    for src, dst, s in ((wg_hbm, wg, 0), (wu_hbm, wu, 1), (wd_hbm, wd, 2)):
        pltpu.make_async_copy(src.at[0], dst, w_sem.at[s]).wait()
    rows = n * R
    kc = 1024
    gacc[...] = jnp.zeros_like(gacc)
    uacc[...] = jnp.zeros_like(uacc)

    def k_step(k, carry):
        ks = pl.ds(pl.multiple_of(k * kc, kc), kc)
        xk = xs[:, :, :, ks].astype(F32).reshape(rows, kc).astype(BF)
        gacc[...] += jnp.dot(xk, wg[ks, :], preferred_element_type=F32)
        uacc[...] += jnp.dot(xk, wu[ks, :], preferred_element_type=F32)
        return carry

    lax.fori_loop(0, D // kc, k_step, 0)
    g = gacc[...]
    hidden = (g / (1.0 + jnp.exp(-g)) * uacc[...]).astype(BF)
    h3[...] = hidden.astype(F32).reshape(chips, 2, R, F)

    mine = place_ref[me].astype(F32)
    info = xs[:, :, :, pl.ds(D, EXTRA)].astype(F32).reshape(rows, EXTRA)
    levels = [info[:, top + k : top + k + 1] for k in range(top)]
    total = functools.reduce(lambda p, q: p + q, levels)
    coef = jnp.zeros((rows, 1), F32)
    for k in range(top):
        coef = coef + jnp.where(info[:, k : k + 1] == mine, route_scale * levels[k] / total, 0.0)
    cf[...] = jnp.broadcast_to(coef, (rows, EXTRA)).reshape(chips, 2, R, EXTRA)

    nc = 1024

    def down_half(cc):
        hh = h3[:, cc].reshape(chips * R, F).astype(BF)
        scale = cf[:, cc].reshape(chips * R, EXTRA)[:, :1]

        def n_step(k, carry):
            ns = pl.ds(pl.multiple_of(k * nc, nc), nc)
            p = jnp.dot(hh, wd[:, ns], preferred_element_type=F32).astype(BF).astype(F32)
            acc[:, cc, :, ns] = (p * scale).reshape(chips, R, nc).astype(BF)
            return carry

        lax.fori_loop(0, D // nc, n_step, 0)

    def to_core(i):
        return pltpu.make_async_remote_copy(
            acc.at[i, 1 - c], rc.at[i], rs_ss.at[CORE, i], rc_s.at[i], device_id={"expert": peer_c}
        )

    def to_b(zz, aa):
        i = at(zz, aa, 1 - b)
        return pltpu.make_async_remote_copy(
            acc.at[i, c], rb.at[zz, aa], rs_ss.at[SIDE_B, i], rb_s.at[zz, aa], device_id={"expert": peer_b}
        )

    def to_a(zz):
        i = at(zz, 1 - a, b)
        return pltpu.make_async_remote_copy(
            acc.at[i, c], ra.at[zz], rs_ss.at[SIDE_A, i], ra_s.at[zz], device_id={"expert": peer_a}
        )

    def to_up(zz):
        i = at(zz, a, b)
        return pltpu.make_async_remote_copy(
            acc.at[i, c], ru.at[zz], rs_ss.at[UP, i], ru_s.at[zz], device_id={"expert": up}
        )

    def to_down(zz):
        i = at(zz, a, b)
        return pltpu.make_async_remote_copy(
            acc.at[i, c], rd.at[zz], rs_ss.at[DOWN, i], rd_s.at[zz], device_id={"expert": down}
        )

    down_half(1 - c)

    def far(k):
        return jnp.where(z < Z // 2, Z - 1 - k, k)

    def core_send(k, carry):
        if planar:
            q = k % (chips // 2)
            zz, other = far(q // 2), 1 - q % 2
            away = 1 - k // (chips // 2)
            aa = (1 - 2 * a) * away + a
            bb = (1 - 2 * b) * other + b
            to_core(at(zz, aa, bb)).start()
        else:
            to_core(far(k)).start()
        return carry

    lax.fori_loop(0, chips, core_send, 0)
    down_half(c)

    def plus(*terms):
        return functools.reduce(lambda p, q: p + q, [t.astype(F32) for t in terms])

    if planar:
        def b_send(k, carry):
            zz = far(k // 2)
            aa = (1 - 2 * a) * (1 - k % 2) + a
            i = at(zz, aa, 1 - b)
            to_core(i).wait_recv()
            acc[i, c] = plus(acc[i, c], rc[i]).astype(BF)
            to_b(zz, aa).start()
            return carry

        lax.fori_loop(0, 2 * Z, b_send, 0)

        def a_send(k, carry):
            zz = far(k)
            i = at(zz, 1 - a, b)
            to_core(i).wait_recv()
            to_b(zz, 1 - a).wait_recv()
            acc[i, c] = plus(acc[i, c], rc[i], rb[zz, 1 - a]).astype(BF)
            to_a(zz).start()
            return carry

        lax.fori_loop(0, Z, a_send, 0)

    def z_send(k, carry):
        zz = far(k)
        i = at(zz, a, b)
        to_core(i).wait_recv()
        if planar:
            to_b(zz, a).wait_recv()
            to_a(zz).wait_recv()
            total = plus(acc[i, c], rc[i], rb[zz, a], ra[zz])
        else:
            total = plus(acc[i, c], rc[i])

        @pl.when(zz > z)
        def _():
            @pl.when(z > 0)
            def _():
                to_up(zz).wait_recv()
                acc[i, c] = (total + ru[zz].astype(F32)).astype(BF)

            @pl.when(z == 0)
            def _():
                acc[i, c] = total.astype(BF)

            to_up(zz).start()

        @pl.when(zz < z)
        def _():
            @pl.when(z < Z - 1)
            def _():
                to_down(zz).wait_recv()
                acc[i, c] = (total + rd[zz].astype(F32)).astype(BF)

            @pl.when(z == Z - 1)
            def _():
                acc[i, c] = total.astype(BF)

            to_down(zz).start()

        @pl.when(zz == z)
        def _():
            acc[i, c] = total.astype(BF)

        return carry

    lax.fori_loop(0, Z, z_send, 0)

    @pl.when(z == 0)
    def _():
        to_down(z).wait_recv()
        moe_ref[...] = plus(acc[chip, c], rd[z]).astype(BF)

    @pl.when(z == Z - 1)
    def _():
        to_up(z).wait_recv()
        moe_ref[...] = plus(acc[chip, c], ru[z]).astype(BF)

    @pl.when((z > 0) & (z < Z - 1))
    def _():
        to_up(z).wait_recv()
        to_down(z).wait_recv()
        moe_ref[...] = plus(acc[chip, c], ru[z], rd[z]).astype(BF)

    def core_done(i, carry):
        ag(i, c, CORE, peer_c).wait_send()
        to_core(i).wait_send()
        return carry

    lax.fori_loop(0, chips, core_done, 0)

    def z_done(zz, carry):
        i = at(zz, a, b)
        pl.when((zz <= z) & (z < Z - 1))(lambda: ag(i, c, UP, up).wait_send())
        pl.when((zz >= z) & (z > 0))(lambda: ag(i, c, DOWN, down).wait_send())
        pl.when(zz > z)(lambda: to_up(zz).wait_send())
        pl.when(zz < z)(lambda: to_down(zz).wait_send())
        if planar:
            ag(i, c, SIDE_A, peer_a).wait_send()
            to_a(zz).wait_send()
            for aa in range(2):
                ag(at(zz, aa, b), c, SIDE_B, peer_b).wait_send()
                to_b(zz, aa).wait_send()
        return carry

    lax.fori_loop(0, Z, z_done, 0)


def per_device(
    normed, expert_ids, gate_levels, placement, w_gate, w_up, w_down,
    q_latent, q_rope, cache_latent, cache_rope, lengths,
):
    n = lax.axis_size("expert")
    Z, Y, X = chip_grid(n)
    chips = n // 2
    R, D = normed.shape
    F = w_gate.shape[2]
    heads = q_latent.shape[1]
    vmem = pl.BlockSpec(memory_space=pltpu.VMEM)
    smem = pl.BlockSpec(memory_space=pltpu.SMEM)
    hbm = pl.BlockSpec(memory_space=pl.ANY)
    dma = pltpu.SemaphoreType.DMA
    side = Z if Y * X > 1 else 1
    return pl.pallas_call(
        functools.partial(body, n),
        out_shape=(
            jax.ShapeDtypeStruct((R, D), BF),
            jax.ShapeDtypeStruct(q_latent.shape, BF),
        ),
        in_specs=[vmem, vmem, vmem, smem, smem, hbm, hbm, hbm, vmem, vmem, vmem, vmem],
        out_specs=(vmem, vmem),
        scratch_shapes=[
            pltpu.VMEM((chips, 2, R, D + EXTRA), BF),
            pltpu.VMEM((chips, 2, R, D), BF),
            pltpu.VMEM((chips, R, D), BF),
            pltpu.VMEM((side, 2, R, D), BF),
            pltpu.VMEM((side, R, D), BF),
            pltpu.VMEM((Z, R, D), BF),
            pltpu.VMEM((Z, R, D), BF),
            pltpu.VMEM((D, F), BF),
            pltpu.VMEM((D, F), BF),
            pltpu.VMEM((F, D), BF),
            pltpu.VMEM((chips, 2, R, F), F32),
            pltpu.VMEM((chips, 2, R, EXTRA), F32),
            pltpu.VMEM((heads * R, 128), F32),
            pltpu.VMEM((n * R, F), F32),
            pltpu.VMEM((n * R, F), F32),
            dma((3,)),
            dma((5, chips)),
            dma((chips, 2)),
            dma((5, chips)),
            dma((chips,)),
            dma((side, 2)),
            dma((side,)),
            dma((Z,)),
            dma((Z,)),
        ],
        compiler_params=pltpu.CompilerParams(
            collective_id=0, has_side_effects=True, vmem_limit_bytes=60 << 20
        ),
        cost_estimate=pl.CostEstimate(flops=3 * 10**9, bytes_accessed=13 * 10**6, transcendentals=300000),
    )(
        normed, expert_ids, gate_levels, lengths, placement, w_gate, w_up, w_down,
        q_latent, q_rope, cache_latent, cache_rope,
    )


def solution(mesh):
    rows = ("groups", "expert")
    in_specs = (
        P(rows, None), P(rows, None), P(rows, None), P(),
        P("expert", None, None), P("expert", None, None), P("expert", None, None),
        P(rows, None, None), P(rows, None), P(rows, None, None), P(rows, None, None), P(rows),
    )
    out_specs = (P(rows, None), P(rows, None, None))
    return jax.shard_map(
        per_device, mesh=mesh, in_specs=in_specs, out_specs=out_specs, check_vma=False
    )
```

```python
import functools

import jax
import jax.numpy as jnp
from jax import lax
from jax.experimental import pallas as pl
from jax.experimental.pallas import tpu as pltpu
from jax.sharding import PartitionSpec as P

score_scale = 192.0 ** (-0.5)
route_scale = 2.5
BF, F32 = jnp.bfloat16, jnp.float32
EXTRA = 128
SIDE_A, SIDE_B, CORE = range(3)


def chip_grid(n):
    return (4, 2, 2) if n == 32 else (n // 2, 1, 1)


def body(
    n,
    normed_ref, ids_ref, lev_ref, len_ref, place_ref, wg_hbm, wu_hbm, wd_hbm,
    ql_ref, qr_ref, cl_ref, cr_ref,
    moe_ref, att_ref,
    xs, acc, rc, rb, ra, rz, wg, wu, wd, h3, cf, rq, gacc, uacc,
    w_sem, ag_ss, ag_rs, agz_ss, rs_ss, rsz_ss, rc_s, rb_s, ra_s, rz_s,
):
    Z, Y, X = chip_grid(n)
    plane = Y * X
    planar = plane > 1
    chips = n // 2
    R, D = normed_ref.shape
    F = wg.shape[1]
    top = ids_ref.shape[0]
    me = lax.axis_index("expert")
    c = me % 2
    chip = me // 2
    z = chip // plane
    y = (chip % plane) // X
    x = chip % X
    a = x * (1 - c) + y * c
    b = y * (1 - c) + x * c
    sa = (1 - c) + X * c
    sb = X * (1 - c) + c
    peer_a = me + 2 * (1 - 2 * a) * sa
    peer_b = me + 2 * (1 - 2 * b) * sb
    peer_c = 2 * chip + 1 - c

    def at(zz, aa, bb):
        if planar:
            return zz * plane + aa * sa + bb * sb
        return zz

    for src, dst, s in ((wg_hbm, wg, 0), (wu_hbm, wu, 1), (wd_hbm, wd, 2)):
        pltpu.make_async_copy(src.at[0], dst, w_sem.at[s]).start()

    xs[chip, c, :, pl.ds(0, D)] = normed_ref[...]
    lane = lax.broadcasted_iota(jnp.int32, (R, EXTRA), 1)
    same = lax.broadcasted_iota(jnp.int32, (R, R), 0) == lax.broadcasted_iota(jnp.int32, (R, R), 1)

    def column(ref, k):
        row = jnp.broadcast_to(ref[k : k + 1, :].astype(F32), (R, R))
        return jnp.sum(jnp.where(same, row, 0.0), axis=1, keepdims=True)

    tail = jnp.zeros((R, EXTRA), F32)
    for k in range(top):
        tail = jnp.where(lane == k, column(ids_ref, k), tail)
        tail = jnp.where(lane == top + k, column(lev_ref, k), tail)
    xs[chip, c, :, pl.ds(D, EXTRA)] = tail.astype(BF)

    barrier = pltpu.get_barrier_semaphore()

    def greet(dev):
        pl.semaphore_signal(barrier, inc=1, device_id={"expert": dev})

    greet(peer_c)
    if planar:
        greet(peer_a)
        greet(peer_b)
    for d in range(1, Z):
        greet(me + 2 * plane * ((z + d) % Z - z))
    pl.semaphore_wait(barrier, Z - 1 + (3 if planar else 1))

    def ag(i, cc, way, dev):
        return pltpu.make_async_remote_copy(
            xs.at[i, cc], xs.at[i, cc], ag_ss.at[way, i], ag_rs.at[i, cc], device_id={"expert": dev}
        )

    def got(i, cc):
        ag(i, cc, CORE, peer_c).wait_recv()

    def share(i):
        if planar:
            ag(i, c, SIDE_A, peer_a).start()
            ag(i, c, SIDE_B, peer_b).start()
        ag(i, c, CORE, peer_c).start()

    def column_dev(zz):
        return me + 2 * plane * (zz - z)

    def ag_z(zz):
        return pltpu.make_async_remote_copy(
            xs.at[chip, c], xs.at[chip, c], agz_ss.at[zz], ag_rs.at[chip, c],
            device_id={"expert": column_dev(zz)},
        )

    share(chip)

    def z_out(d, carry):
        pl.when(z - d >= 0)(lambda: ag_z(z - d).start())
        pl.when(z + d < Z)(lambda: ag_z(z + d).start())
        return carry

    lax.fori_loop(1, Z, z_out, 0)

    qr = qr_ref[...].astype(F32)
    heads, rope = ql_ref.shape[1], cr_ref.shape[1]
    for h in range(heads):
        rq[h * R : (h + 1) * R, :rope] = qr[:, h * rope : (h + 1) * rope]

    lmax = cl_ref.shape[1]

    def attend(t):
        keys = cl_ref[t]
        rope_q = rq[pl.ds(t, heads, stride=R), :rope].astype(BF)
        s = lax.dot_general(ql_ref[t], keys, (((1,), (1,)), ((), ())), preferred_element_type=F32)
        s = s + jnp.dot(rope_q, cr_ref[t], preferred_element_type=F32)
        s = s * score_scale
        seen = lax.broadcasted_iota(jnp.int32, (heads, lmax), 1) < len_ref[t]
        s = jnp.where(seen, s, -1e30)
        e = jnp.where(seen, jnp.exp(s - jnp.max(s, axis=-1, keepdims=True)), 0.0)
        p = (e / jnp.sum(e, axis=-1, keepdims=True)).astype(BF)
        att_ref[t] = jnp.dot(p, keys, preferred_element_type=F32).astype(BF)

    def from_a(zz):
        i = at(zz, 1 - a, b)
        got(i, c)
        ag(i, c, SIDE_B, peer_b).start()
        ag(i, c, CORE, peer_c).start()

    if planar:
        from_a(z)

    def z_step(d, carry):
        @pl.when(z - d >= 0)
        def _():
            i = at(z - d, a, b)
            got(i, c)
            share(i)

        @pl.when(z + d < Z)
        def _():
            i = at(z + d, a, b)
            got(i, c)
            share(i)

        if planar:
            pl.when(z - d >= 0)(lambda: from_a(z - d))
            pl.when(z + d < Z)(lambda: from_a(z + d))
        return carry

    lax.fori_loop(1, Z, z_step, 0)

    if planar:
        def from_b(k, carry):
            attend(k)
            i = at((z + k // 2) % Z, k % 2, 1 - b)
            got(i, c)
            ag(i, c, CORE, peer_c).start()
            return carry

        lax.fori_loop(0, 2 * Z, from_b, 0)
        first = min(2 * Z, R)
    else:
        first = 0
    for t in range(first, R):
        attend(t)

    def from_core(i, carry):
        got(i, 1 - c)
        return carry

    lax.fori_loop(0, chips, from_core, 0)

    for src, dst, s in ((wg_hbm, wg, 0), (wu_hbm, wu, 1), (wd_hbm, wd, 2)):
        pltpu.make_async_copy(src.at[0], dst, w_sem.at[s]).wait()
    rows = n * R
    kc = 1024
    gacc[...] = jnp.zeros_like(gacc)
    uacc[...] = jnp.zeros_like(uacc)

    def k_step(k, carry):
        ks = pl.ds(pl.multiple_of(k * kc, kc), kc)
        xk = xs[:, :, :, ks].astype(F32).reshape(rows, kc).astype(BF)
        gacc[...] += jnp.dot(xk, wg[ks, :], preferred_element_type=F32)
        uacc[...] += jnp.dot(xk, wu[ks, :], preferred_element_type=F32)
        return carry

    lax.fori_loop(0, D // kc, k_step, 0)
    g = gacc[...]
    hidden = (g / (1.0 + jnp.exp(-g)) * uacc[...]).astype(BF)
    h3[...] = hidden.astype(F32).reshape(chips, 2, R, F)

    mine = place_ref[me].astype(F32)
    info = xs[:, :, :, pl.ds(D, EXTRA)].astype(F32).reshape(rows, EXTRA)
    levels = [info[:, top + k : top + k + 1] for k in range(top)]
    total = functools.reduce(lambda p, q: p + q, levels)
    coef = jnp.zeros((rows, 1), F32)
    for k in range(top):
        coef = coef + jnp.where(info[:, k : k + 1] == mine, route_scale * levels[k] / total, 0.0)
    cf[...] = jnp.broadcast_to(coef, (rows, EXTRA)).reshape(chips, 2, R, EXTRA)

    nc = 1024

    def down_half(cc):
        hh = h3[:, cc].reshape(chips * R, F).astype(BF)
        scale = cf[:, cc].reshape(chips * R, EXTRA)[:, :1]

        def n_step(k, carry):
            ns = pl.ds(pl.multiple_of(k * nc, nc), nc)
            p = jnp.dot(hh, wd[:, ns], preferred_element_type=F32).astype(BF).astype(F32)
            acc[:, cc, :, ns] = (p * scale).reshape(chips, R, nc).astype(BF)
            return carry

        lax.fori_loop(0, D // nc, n_step, 0)

    def to_core(i):
        return pltpu.make_async_remote_copy(
            acc.at[i, 1 - c], rc.at[i], rs_ss.at[CORE, i], rc_s.at[i], device_id={"expert": peer_c}
        )

    def to_b(zz, aa):
        i = at(zz, aa, 1 - b)
        return pltpu.make_async_remote_copy(
            acc.at[i, c], rb.at[zz, aa], rs_ss.at[SIDE_B, i], rb_s.at[zz, aa], device_id={"expert": peer_b}
        )

    def to_a(zz):
        i = at(zz, 1 - a, b)
        return pltpu.make_async_remote_copy(
            acc.at[i, c], ra.at[zz], rs_ss.at[SIDE_A, i], ra_s.at[zz], device_id={"expert": peer_a}
        )

    def to_z(zz):
        return pltpu.make_async_remote_copy(
            acc.at[at(zz, a, b), c], rz.at[z], rsz_ss.at[zz], rz_s.at[z],
            device_id={"expert": column_dev(zz)},
        )

    def from_z(zz):
        return pltpu.make_async_remote_copy(
            acc.at[chip, c], rz.at[zz], rsz_ss.at[zz], rz_s.at[zz],
            device_id={"expert": column_dev(zz)},
        )

    down_half(1 - c)

    def far(k):
        return (z + 1 + k) % Z

    def core_send(k, carry):
        if planar:
            q = k % (chips // 2)
            zz, other = far(q // 2), 1 - q % 2
            away = 1 - k // (chips // 2)
            aa = (1 - 2 * a) * away + a
            bb = (1 - 2 * b) * other + b
            to_core(at(zz, aa, bb)).start()
        else:
            to_core(far(k)).start()
        return carry

    lax.fori_loop(0, chips, core_send, 0)
    down_half(c)

    def plus(*terms):
        return functools.reduce(lambda p, q: p + q, [t.astype(F32) for t in terms])

    if planar:
        def b_send(k, carry):
            zz = far(k // 2)
            aa = (1 - 2 * a) * (1 - k % 2) + a
            i = at(zz, aa, 1 - b)
            to_core(i).wait_recv()
            acc[i, c] = plus(acc[i, c], rc[i]).astype(BF)
            to_b(zz, aa).start()
            return carry

        lax.fori_loop(0, 2 * Z, b_send, 0)

        def a_send(k):
            zz = far(k)
            i = at(zz, 1 - a, b)
            to_core(i).wait_recv()
            to_b(zz, 1 - a).wait_recv()
            acc[i, c] = plus(acc[i, c], rc[i], rb[zz, 1 - a]).astype(BF)
            to_a(zz).start()

        a_send(0)

    def column_sum(zz):
        i = at(zz, a, b)
        to_core(i).wait_recv()
        if planar:
            to_b(zz, a).wait_recv()
            to_a(zz).wait_recv()
            return plus(acc[i, c], rc[i], rb[zz, a], ra[zz])
        return plus(acc[i, c], rc[i])

    def z_send(k, carry):
        if planar:
            a_send(k + 1)
        zz = far(k)
        acc[at(zz, a, b), c] = column_sum(zz).astype(BF)
        to_z(zz).start()
        return carry

    lax.fori_loop(0, Z - 1, z_send, 0)
    result = column_sum(z)
    for d in range(1, Z):
        zz = (z + d) % Z
        from_z(zz).wait_recv()
        result = result + rz[zz].astype(F32)
    moe_ref[...] = result.astype(BF)

    def core_done(i, carry):
        ag(i, c, CORE, peer_c).wait_send()
        to_core(i).wait_send()
        return carry

    lax.fori_loop(0, chips, core_done, 0)

    def z_done(zz, carry):
        i = at(zz, a, b)

        @pl.when(zz != z)
        def _():
            ag_z(zz).wait_send()
            to_z(zz).wait_send()

        if planar:
            ag(i, c, SIDE_A, peer_a).wait_send()
            to_a(zz).wait_send()
            for aa in range(2):
                ag(at(zz, aa, b), c, SIDE_B, peer_b).wait_send()
                to_b(zz, aa).wait_send()
        return carry

    lax.fori_loop(0, Z, z_done, 0)


def per_device(
    normed, expert_ids, gate_levels, placement, w_gate, w_up, w_down,
    q_latent, q_rope, cache_latent, cache_rope, lengths,
):
    n = lax.axis_size("expert")
    Z, Y, X = chip_grid(n)
    chips = n // 2
    R, D = normed.shape
    F = w_gate.shape[2]
    heads = q_latent.shape[1]
    vmem = pl.BlockSpec(memory_space=pltpu.VMEM)
    smem = pl.BlockSpec(memory_space=pltpu.SMEM)
    hbm = pl.BlockSpec(memory_space=pl.ANY)
    dma = pltpu.SemaphoreType.DMA
    side = Z if Y * X > 1 else 1
    return pl.pallas_call(
        functools.partial(body, n),
        out_shape=(
            jax.ShapeDtypeStruct((R, D), BF),
            jax.ShapeDtypeStruct(q_latent.shape, BF),
        ),
        in_specs=[vmem, vmem, vmem, smem, smem, hbm, hbm, hbm, vmem, vmem, vmem, vmem],
        out_specs=(vmem, vmem),
        scratch_shapes=[
            pltpu.VMEM((chips, 2, R, D + EXTRA), BF),
            pltpu.VMEM((chips, 2, R, D), BF),
            pltpu.VMEM((chips, R, D), BF),
            pltpu.VMEM((side, 2, R, D), BF),
            pltpu.VMEM((side, R, D), BF),
            pltpu.VMEM((Z, R, D), BF),
            pltpu.VMEM((D, F), BF),
            pltpu.VMEM((D, F), BF),
            pltpu.VMEM((F, D), BF),
            pltpu.VMEM((chips, 2, R, F), F32),
            pltpu.VMEM((chips, 2, R, EXTRA), F32),
            pltpu.VMEM((heads * R, 128), F32),
            pltpu.VMEM((n * R, F), F32),
            pltpu.VMEM((n * R, F), F32),
            dma((3,)),
            dma((3, chips)),
            dma((chips, 2)),
            dma((Z,)),
            dma((3, chips)),
            dma((Z,)),
            dma((chips,)),
            dma((side, 2)),
            dma((side,)),
            dma((Z,)),
        ],
        compiler_params=pltpu.CompilerParams(
            collective_id=0, has_side_effects=True, vmem_limit_bytes=60 << 20
        ),
        cost_estimate=pl.CostEstimate(flops=3 * 10**9, bytes_accessed=13 * 10**6, transcendentals=300000),
    )(
        normed, expert_ids.T, gate_levels.T, lengths, placement, w_gate, w_up, w_down,
        q_latent, q_rope, cache_latent, cache_rope,
    )


def solution(mesh):
    rows = ("groups", "expert")
    in_specs = (
        P(rows, None), P(rows, None), P(rows, None), P(),
        P("expert", None, None), P("expert", None, None), P("expert", None, None),
        P(rows, None, None), P(rows, None), P(rows, None, None), P(rows, None, None), P(rows),
    )
    out_specs = (P(rows, None), P(rows, None, None))
    return jax.shard_map(
        per_device, mesh=mesh, in_specs=in_specs, out_specs=out_specs, check_vma=False
    )
```

```python
import functools

import jax
import jax.numpy as jnp
from jax import lax
from jax.experimental import pallas as pl
from jax.experimental.pallas import tpu as pltpu
from jax.sharding import PartitionSpec as P

score_scale = 192.0 ** (-0.5)
route_scale = 2.5
BF, F32 = jnp.bfloat16, jnp.float32
EXTRA = 128
PA, PR = 3, 2
SIDE_A, SIDE_B = range(2)


def chip_grid(n):
    return (4, 2, 2) if n == 32 else (n // 2, 1, 1)


def parts(cols, most):
    return max(p for p in range(1, most + 1) if cols % (128 * p) == 0)


def body(
    n,
    normed_ref, ids_ref, lev_ref, len_ref, place_ref, wg_hbm, wu_hbm, wd_hbm,
    ql_hbm, qr_ref, cl_hbm, cr_hbm,
    moe_ref, att_hbm,
    xs, acc, rc, rb, ra, rz, wg, wu, wd, h3, cf, rq, gacc, uacc, ql_ref, cl_ref, cr_ref, att_ref,
    w_sem, in_sem, out_sem, ag_ss, ag_rs, agz_ss, agc_ss, agc_rs, rs_ss, rsz_ss, rsc_ss, rc_s, rb_s, ra_s, rz_s,
):
    Z, Y, X = chip_grid(n)
    plane = Y * X
    planar = plane > 1
    chips = n // 2
    R, D = normed_ref.shape
    F = wg.shape[1]
    top = ids_ref.shape[0]
    me = lax.axis_index("expert")
    c = me % 2
    chip = me // 2
    z = chip // plane
    y = (chip % plane) // X
    x = chip % X
    a = x * (1 - c) + y * c
    b = y * (1 - c) + x * c
    sa = (1 - c) + X * c
    sb = X * (1 - c) + c
    peer_a = me + 2 * (1 - 2 * a) * sa
    peer_b = me + 2 * (1 - 2 * b) * sb
    peer_c = 2 * chip + 1 - c

    def at(zz, aa, bb):
        if planar:
            return zz * plane + aa * sa + bb * sb
        return zz

    barrier = pltpu.get_barrier_semaphore()

    def greet(dev):
        pl.semaphore_signal(barrier, inc=1, device_id={"expert": dev})

    greet(peer_c)
    if planar:
        greet(peer_a)
        greet(peer_b)
    for d in range(1, Z):
        greet(me + 2 * plane * ((z + d) % Z - z))
    for src, dst, s in ((wg_hbm, wg, 0), (wu_hbm, wu, 1), (wd_hbm, wd, 2)):
        pltpu.make_async_copy(src.at[0], dst, w_sem.at[s]).start()

    for k, (src, dst) in enumerate(((ql_hbm, ql_ref), (cl_hbm, cl_ref), (cr_hbm, cr_ref))):
        pltpu.make_async_copy(src, dst, in_sem.at[k]).start()

    xs[chip, c, :, pl.ds(0, D)] = normed_ref[...]
    lane = lax.broadcasted_iota(jnp.int32, (R, EXTRA), 1)
    same = lax.broadcasted_iota(jnp.int32, (R, R), 0) == lax.broadcasted_iota(jnp.int32, (R, R), 1)

    def column(ref, k):
        row = jnp.broadcast_to(ref[k : k + 1, :].astype(F32), (R, R))
        return jnp.sum(jnp.where(same, row, 0.0), axis=1, keepdims=True)

    tail = jnp.zeros((R, EXTRA), F32)
    for k in range(top):
        tail = jnp.where(lane == k, column(ids_ref, k), tail)
        tail = jnp.where(lane == top + k, column(lev_ref, k), tail)
    xs[chip, c, :, pl.ds(D, EXTRA)] = tail.astype(BF)

    pl.semaphore_wait(barrier, Z - 1 + (3 if planar else 1))

    pa = ag_rs.shape[1]
    wa = (D + EXTRA) // pa

    def ag(i, p, way, dev):
        part = xs.at[i, c, :, pl.ds(p * wa, wa)]
        return pltpu.make_async_remote_copy(
            part, part, ag_ss.at[way, i, p], ag_rs.at[i, p], device_id={"expert": dev}
        )

    def ag_core(i, cc):
        return pltpu.make_async_remote_copy(
            xs.at[i, cc], xs.at[i, cc], agc_ss.at[i], agc_rs.at[i], device_id={"expert": peer_c}
        )

    def got(i, p):
        ag(i, p, SIDE_A, peer_a).wait_recv()

    def ag_z(zz, p, way, dev):
        i = at(zz, a, b)
        part = xs.at[i, c, :, pl.ds(p * wa, wa)]
        return pltpu.make_async_remote_copy(
            part, part, agz_ss.at[way, zz, p], ag_rs.at[i, p], device_id={"expert": dev}
        )

    def go_up(zz, p):
        pl.when(z < Z - 1)(lambda: ag_z(zz, p, 0, me + 2 * plane).start())

    def go_down(zz, p):
        pl.when(z > 0)(lambda: ag_z(zz, p, 1, me - 2 * plane).start())

    def share(zz, wait, *onward):
        i = at(zz, a, b)
        for p in range(pa):
            if wait:
                got(i, p)
            for step in onward:
                step(zz, p)
            if planar:
                ag(i, p, SIDE_A, peer_a).start()
                ag(i, p, SIDE_B, peer_b).start()
        ag_core(i, c).start()

    def column_dev(zz):
        return me + 2 * plane * (zz - z)

    share(z, False, go_up, go_down)

    qr = qr_ref[...].astype(F32)
    heads, rope = ql_ref.shape[1], cr_ref.shape[1]
    for h in range(heads):
        rq[h * R : (h + 1) * R, :rope] = qr[:, h * rope : (h + 1) * rope]

    lmax = cl_ref.shape[1]
    for k, (src, dst) in enumerate(((ql_hbm, ql_ref), (cl_hbm, cl_ref), (cr_hbm, cr_ref))):
        pltpu.make_async_copy(src, dst, in_sem.at[k]).wait()

    def attend(t):
        keys = cl_ref[t]
        rope_q = rq[pl.ds(t, heads, stride=R), :rope].astype(BF)
        s = lax.dot_general(ql_ref[t], keys, (((1,), (1,)), ((), ())), preferred_element_type=F32)
        s = s + jnp.dot(rope_q, cr_ref[t], preferred_element_type=F32)
        s = s * score_scale
        seen = lax.broadcasted_iota(jnp.int32, (heads, lmax), 1) < len_ref[t]
        s = jnp.where(seen, s, -1e30)
        e = jnp.where(seen, jnp.exp(s - jnp.max(s, axis=-1, keepdims=True)), 0.0)
        p = (e / jnp.sum(e, axis=-1, keepdims=True)).astype(BF)
        att_ref[t] = jnp.dot(p, keys, preferred_element_type=F32).astype(BF)

    def from_a(zz):
        i = at(zz, 1 - a, b)
        for p in range(pa):
            got(i, p)
            ag(i, p, SIDE_B, peer_b).start()
        ag_core(i, c).start()

    if planar:
        from_a(z)

    def z_step(d, carry):
        pl.when(z - d >= 0)(lambda: share(z - d, True, go_up))
        pl.when(z + d < Z)(lambda: share(z + d, True, go_down))
        if planar:
            pl.when(z - d >= 0)(lambda: from_a(z - d))
            pl.when(z + d < Z)(lambda: from_a(z + d))
        return carry

    lax.fori_loop(1, Z, z_step, 0)

    if planar:
        def from_b(k, carry):
            attend(k)
            i = at((z + k // 2) % Z, k % 2, 1 - b)
            for p in range(pa):
                got(i, p)
            ag_core(i, c).start()
            return carry

        lax.fori_loop(0, 2 * Z, from_b, 0)
        first = min(2 * Z, R)
    else:
        first = 0
    for t in range(first, R):
        attend(t)

    pltpu.make_async_copy(att_ref, att_hbm, out_sem).start()

    def from_core(i, carry):
        ag_core(i, 1 - c).wait_recv()
        return carry

    lax.fori_loop(0, chips, from_core, 0)

    for src, dst, s in ((wg_hbm, wg, 0), (wu_hbm, wu, 1), (wd_hbm, wd, 2)):
        pltpu.make_async_copy(src.at[0], dst, w_sem.at[s]).wait()
    rows = n * R
    kc = 1024
    gacc[...] = jnp.zeros_like(gacc)
    uacc[...] = jnp.zeros_like(uacc)

    def k_step(k, carry):
        ks = pl.ds(pl.multiple_of(k * kc, kc), kc)
        xk = xs[:, :, :, ks].astype(F32).reshape(rows, kc).astype(BF)
        gacc[...] += jnp.dot(xk, wg[ks, :], preferred_element_type=F32)
        uacc[...] += jnp.dot(xk, wu[ks, :], preferred_element_type=F32)
        return carry

    lax.fori_loop(0, D // kc, k_step, 0)
    g = gacc[...]
    hidden = (g / (1.0 + jnp.exp(-g)) * uacc[...]).astype(BF)
    h3[...] = hidden.astype(F32).reshape(chips, 2, R, F)

    mine = place_ref[me].astype(F32)
    info = xs[:, :, :, pl.ds(D, EXTRA)].astype(F32).reshape(rows, EXTRA)
    levels = [info[:, top + k : top + k + 1] for k in range(top)]
    total = functools.reduce(lambda p, q: p + q, levels)
    coef = jnp.zeros((rows, 1), F32)
    for k in range(top):
        coef = coef + jnp.where(info[:, k : k + 1] == mine, route_scale * levels[k] / total, 0.0)
    cf[...] = jnp.broadcast_to(coef, (rows, EXTRA)).reshape(chips, 2, R, EXTRA)

    nc = 1024

    def down_half(cc):
        hh = h3[:, cc].reshape(chips * R, F).astype(BF)
        scale = cf[:, cc].reshape(chips * R, EXTRA)[:, :1]

        def n_step(k, carry):
            ns = pl.ds(pl.multiple_of(k * nc, nc), nc)
            p = jnp.dot(hh, wd[:, ns], preferred_element_type=F32).astype(BF).astype(F32)
            acc[:, cc, :, ns] = (p * scale).reshape(chips, R, nc).astype(BF)
            return carry

        lax.fori_loop(0, D // nc, n_step, 0)

    pr = rz_s.shape[1]
    wr = D // pr

    def cols(p):
        return pl.ds(p * wr, wr)

    def to_core(i):
        return pltpu.make_async_remote_copy(
            acc.at[i, 1 - c], rc.at[i], rsc_ss.at[i], rc_s.at[i], device_id={"expert": peer_c}
        )

    def to_b(zz, aa, p):
        i = at(zz, aa, 1 - b)
        return pltpu.make_async_remote_copy(
            acc.at[i, c, :, cols(p)], rb.at[zz, aa, :, cols(p)], rs_ss.at[SIDE_B, i, p],
            rb_s.at[zz, aa, p], device_id={"expert": peer_b},
        )

    def to_a(zz, p):
        i = at(zz, 1 - a, b)
        return pltpu.make_async_remote_copy(
            acc.at[i, c, :, cols(p)], ra.at[zz, :, cols(p)], rs_ss.at[SIDE_A, i, p],
            ra_s.at[zz, p], device_id={"expert": peer_a},
        )

    def to_z(zz, p):
        return pltpu.make_async_remote_copy(
            acc.at[at(zz, a, b), c, :, cols(p)], rz.at[z, :, cols(p)], rsz_ss.at[zz, p],
            rz_s.at[z, p], device_id={"expert": column_dev(zz)},
        )

    def from_z(zz, p):
        return pltpu.make_async_remote_copy(
            acc.at[chip, c, :, cols(p)], rz.at[zz, :, cols(p)], rsz_ss.at[zz, p],
            rz_s.at[zz, p], device_id={"expert": column_dev(zz)},
        )

    down_half(1 - c)

    def far(k):
        return (z + 1 + k) % Z

    def core_send(k, carry):
        if planar:
            q = k % (chips // 2)
            zz, other = far(q // 2), 1 - q % 2
            away = 1 - k // (chips // 2)
            aa = (1 - 2 * a) * away + a
            bb = (1 - 2 * b) * other + b
            to_core(at(zz, aa, bb)).start()
        else:
            to_core(far(k)).start()
        return carry

    lax.fori_loop(0, chips, core_send, 0)
    down_half(c)

    def plus(*terms):
        return functools.reduce(lambda p, q: p + q, [t.astype(F32) for t in terms])

    if planar:
        def b_send(k, carry):
            zz = far(k // 2)
            aa = (1 - 2 * a) * (1 - k % 2) + a
            i = at(zz, aa, 1 - b)
            to_core(i).wait_recv()
            acc[i, c] = plus(acc[i, c], rc[i]).astype(BF)
            for p in range(pr):
                to_b(zz, aa, p).start()
            return carry

        lax.fori_loop(0, 2 * Z, b_send, 0)

        def a_send(k):
            zz = far(k)
            i = at(zz, 1 - a, b)
            to_core(i).wait_recv()
            for p in range(pr):
                to_b(zz, 1 - a, p).wait_recv()
                cp = cols(p)
                acc[i, c, :, cp] = plus(acc[i, c, :, cp], rc[i, :, cp], rb[zz, 1 - a, :, cp]).astype(BF)
                to_a(zz, p).start()

        a_send(0)

    def column_sum(zz, p):
        i = at(zz, a, b)
        cp = cols(p)
        if planar:
            to_b(zz, a, p).wait_recv()
            to_a(zz, p).wait_recv()
            return plus(acc[i, c, :, cp], rc[i, :, cp], rb[zz, a, :, cp], ra[zz, :, cp])
        return plus(acc[i, c, :, cp], rc[i, :, cp])

    def z_send(k, carry):
        if planar:
            a_send(k + 1)
        zz = far(k)
        to_core(at(zz, a, b)).wait_recv()
        for p in range(pr):
            acc[at(zz, a, b), c, :, cols(p)] = column_sum(zz, p).astype(BF)
            to_z(zz, p).start()
        return carry

    lax.fori_loop(0, Z - 1, z_send, 0)
    to_core(chip).wait_recv()
    for p in range(pr):
        result = column_sum(z, p)
        for d in range(1, Z):
            zz = (z + d) % Z
            from_z(zz, p).wait_recv()
            result = result + rz[zz, :, cols(p)].astype(F32)
        moe_ref[:, cols(p)] = result.astype(BF)

    pltpu.make_async_copy(att_ref, att_hbm, out_sem).wait()

    def core_done(i, carry):
        ag_core(i, c).wait_send()
        to_core(i).wait_send()
        return carry

    lax.fori_loop(0, chips, core_done, 0)

    def z_done(zz, carry):
        i = at(zz, a, b)

        @pl.when(zz != z)
        def _():
            for p in range(pr):
                to_z(zz, p).wait_send()

        for p in range(pa):
            pl.when((zz <= z) & (z < Z - 1))(lambda: ag_z(zz, p, 0, me + 2 * plane).wait_send())
            pl.when((zz >= z) & (z > 0))(lambda: ag_z(zz, p, 1, me - 2 * plane).wait_send())
        if planar:
            for p in range(pa):
                ag(i, p, SIDE_A, peer_a).wait_send()
                for aa in range(2):
                    ag(at(zz, aa, b), p, SIDE_B, peer_b).wait_send()
            for p in range(pr):
                to_a(zz, p).wait_send()
                for aa in range(2):
                    to_b(zz, aa, p).wait_send()
        return carry

    lax.fori_loop(0, Z, z_done, 0)


def per_device(
    normed, expert_ids, gate_levels, placement, w_gate, w_up, w_down,
    q_latent, q_rope, cache_latent, cache_rope, lengths,
):
    n = lax.axis_size("expert")
    Z, Y, X = chip_grid(n)
    chips = n // 2
    R, D = normed.shape
    F = w_gate.shape[2]
    heads = q_latent.shape[1]
    vmem = pl.BlockSpec(memory_space=pltpu.VMEM)
    smem = pl.BlockSpec(memory_space=pltpu.SMEM)
    hbm = pl.BlockSpec(memory_space=pl.ANY)
    dma = pltpu.SemaphoreType.DMA
    side = Z if Y * X > 1 else 1
    pa, pr = parts(D + EXTRA, PA), parts(D, PR)
    return pl.pallas_call(
        functools.partial(body, n),
        out_shape=(
            jax.ShapeDtypeStruct((R, D), BF),
            jax.ShapeDtypeStruct(q_latent.shape, BF),
        ),
        in_specs=[vmem, vmem, vmem, smem, smem, hbm, hbm, hbm, hbm, vmem, hbm, hbm],
        out_specs=(vmem, hbm),
        scratch_shapes=[
            pltpu.VMEM((chips, 2, R, D + EXTRA), BF),
            pltpu.VMEM((chips, 2, R, D), BF),
            pltpu.VMEM((chips, R, D), BF),
            pltpu.VMEM((side, 2, R, D), BF),
            pltpu.VMEM((side, R, D), BF),
            pltpu.VMEM((Z, R, D), BF),
            pltpu.VMEM((D, F), BF),
            pltpu.VMEM((D, F), BF),
            pltpu.VMEM((F, D), BF),
            pltpu.VMEM((chips, 2, R, F), F32),
            pltpu.VMEM((chips, 2, R, EXTRA), F32),
            pltpu.VMEM((heads * R, 128), F32),
            pltpu.VMEM((n * R, F), F32),
            pltpu.VMEM((n * R, F), F32),
            pltpu.VMEM(q_latent.shape, BF),
            pltpu.VMEM(cache_latent.shape, BF),
            pltpu.VMEM(cache_rope.shape, BF),
            pltpu.VMEM(q_latent.shape, BF),
            dma((3,)),
            dma((3,)),
            dma,
            dma((2, chips, pa)),
            dma((chips, pa)),
            dma((2, Z, pa)),
            dma((chips,)),
            dma((chips,)),
            dma((2, chips, pr)),
            dma((Z, pr)),
            dma((chips,)),
            dma((chips,)),
            dma((side, 2, pr)),
            dma((side, pr)),
            dma((Z, pr)),
        ],
        compiler_params=pltpu.CompilerParams(
            collective_id=0, has_side_effects=True, vmem_limit_bytes=60 << 20
        ),
        cost_estimate=pl.CostEstimate(flops=3 * 10**9, bytes_accessed=13 * 10**6, transcendentals=300000),
    )(
        normed, expert_ids.T, gate_levels.T, lengths, placement, w_gate, w_up, w_down,
        q_latent, q_rope, cache_latent, cache_rope,
    )


def solution(mesh):
    rows = ("groups", "expert")
    in_specs = (
        P(rows, None), P(rows, None), P(rows, None), P(),
        P("expert", None, None), P("expert", None, None), P("expert", None, None),
        P(rows, None, None), P(rows, None), P(rows, None, None), P(rows, None, None), P(rows),
    )
    out_specs = (P(rows, None), P(rows, None, None))
    return jax.shard_map(
        per_device, mesh=mesh, in_specs=in_specs, out_specs=out_specs, check_vma=False
    )
```

```python
import functools

import jax
import jax.numpy as jnp
from jax import lax
from jax.experimental import pallas as pl
from jax.experimental.pallas import tpu as pltpu
from jax.sharding import PartitionSpec as P

score_scale = 192.0 ** (-0.5)
route_scale = 2.5
BF, F32 = jnp.bfloat16, jnp.float32
EXTRA = 128
PA, PR = 3, 2
SIDE_A, SIDE_B = range(2)


def chip_grid(n):
    return (4, 2, 2) if n == 32 else (n // 2, 1, 1)


def parts(cols, most):
    return max(p for p in range(1, most + 1) if cols % (128 * p) == 0)


def body(
    n,
    normed_ref, ids_ref, lev_ref, len_ref, place_ref, wg_hbm, wu_hbm, wd_hbm,
    ql_hbm, qr_ref, cl_hbm, cr_hbm,
    moe_ref, att_hbm,
    xs, acc, rc, rb, ra, rz, wg, wu, wd, h3, cf, rq, gacc, uacc, ql_ref, cl_ref, cr_ref, att_ref,
    w_sem, in_sem, out_sem, ag_ss, ag_rs, agz_ss, agc_ss, agc_rs, rs_ss, rsz_ss, rsc_ss, rc_s, rb_s, ra_s, rz_s,
):
    Z, Y, X = chip_grid(n)
    plane = Y * X
    planar = plane > 1
    chips = n // 2
    R, D = normed_ref.shape
    F = wg.shape[1]
    top = ids_ref.shape[0]
    me = lax.axis_index("expert")
    c = me % 2
    chip = me // 2
    z = chip // plane
    y = (chip % plane) // X
    x = chip % X
    a = x * (1 - c) + y * c
    b = y * (1 - c) + x * c
    sa = (1 - c) + X * c
    sb = X * (1 - c) + c
    peer_a = me + 2 * (1 - 2 * a) * sa
    peer_b = me + 2 * (1 - 2 * b) * sb
    peer_c = 2 * chip + 1 - c

    def at(zz, aa, bb):
        if planar:
            return zz * plane + aa * sa + bb * sb
        return zz

    barrier = pltpu.get_barrier_semaphore()

    def greet(dev):
        pl.semaphore_signal(barrier, inc=1, device_id={"expert": dev})

    greet(peer_c)
    if planar:
        greet(peer_a)
        greet(peer_b)
    for d in range(1, Z):
        greet(me + 2 * plane * ((z + d) % Z - z))
    for src, dst, s in ((wg_hbm, wg, 0), (wu_hbm, wu, 1), (wd_hbm, wd, 2)):
        pltpu.make_async_copy(src.at[0], dst, w_sem.at[s]).start()

    for k, (src, dst) in enumerate(((ql_hbm, ql_ref), (cl_hbm, cl_ref), (cr_hbm, cr_ref))):
        pltpu.make_async_copy(src, dst, in_sem.at[k]).start()

    xs[chip, c, :, pl.ds(0, D)] = normed_ref[...]
    lane = lax.broadcasted_iota(jnp.int32, (R, EXTRA), 1)
    same = lax.broadcasted_iota(jnp.int32, (R, R), 0) == lax.broadcasted_iota(jnp.int32, (R, R), 1)

    def column(ref, k):
        row = jnp.broadcast_to(ref[k : k + 1, :].astype(F32), (R, R))
        return jnp.sum(jnp.where(same, row, 0.0), axis=1, keepdims=True)

    tail = jnp.zeros((R, EXTRA), F32)
    for k in range(top):
        tail = jnp.where(lane == k, column(ids_ref, k), tail)
        tail = jnp.where(lane == top + k, column(lev_ref, k), tail)
    xs[chip, c, :, pl.ds(D, EXTRA)] = tail.astype(BF)

    pl.semaphore_wait(barrier, Z - 1 + (3 if planar else 1))

    pa = ag_rs.shape[1]
    wa = (D + EXTRA) // pa

    def ag(i, p, way, dev):
        part = xs.at[i, c, :, pl.ds(p * wa, wa)]
        return pltpu.make_async_remote_copy(
            part, part, ag_ss.at[way, i, p], ag_rs.at[i, p], device_id={"expert": dev}
        )

    def ag_core(i, cc):
        return pltpu.make_async_remote_copy(
            xs.at[i, cc], xs.at[i, cc], agc_ss.at[i], agc_rs.at[i], device_id={"expert": peer_c}
        )

    def got(i, p):
        ag(i, p, SIDE_A, peer_a).wait_recv()

    def ag_z(zz, p, way, dev):
        i = at(zz, a, b)
        part = xs.at[i, c, :, pl.ds(p * wa, wa)]
        return pltpu.make_async_remote_copy(
            part, part, agz_ss.at[way, zz, p], ag_rs.at[i, p], device_id={"expert": dev}
        )

    def go_up(zz, p):
        pl.when(z < Z - 1)(lambda: ag_z(zz, p, 0, me + 2 * plane).start())

    def go_down(zz, p):
        pl.when(z > 0)(lambda: ag_z(zz, p, 1, me - 2 * plane).start())

    def share(zz, wait, *onward):
        i = at(zz, a, b)
        for p in range(pa):
            if wait:
                got(i, p)
            for step in onward:
                step(zz, p)
            if planar:
                ag(i, p, SIDE_A, peer_a).start()
                ag(i, p, SIDE_B, peer_b).start()
        ag_core(i, c).start()

    def column_dev(zz):
        return me + 2 * plane * (zz - z)

    share(z, False, go_up, go_down)

    qr = qr_ref[...].astype(F32)
    heads, rope = ql_ref.shape[1], cr_ref.shape[1]
    for h in range(heads):
        rq[h * R : (h + 1) * R, :rope] = qr[:, h * rope : (h + 1) * rope]

    lmax = cl_ref.shape[1]
    for k, (src, dst) in enumerate(((ql_hbm, ql_ref), (cl_hbm, cl_ref), (cr_hbm, cr_ref))):
        pltpu.make_async_copy(src, dst, in_sem.at[k]).wait()

    def attend(t):
        keys = cl_ref[t]
        rope_q = rq[pl.ds(t, heads, stride=R), :rope].astype(BF)
        s = lax.dot_general(ql_ref[t], keys, (((1,), (1,)), ((), ())), preferred_element_type=F32)
        s = s + jnp.dot(rope_q, cr_ref[t], preferred_element_type=F32)
        s = s * score_scale
        seen = lax.broadcasted_iota(jnp.int32, (heads, lmax), 1) < len_ref[t]
        s = jnp.where(seen, s, -1e30)
        e = jnp.where(seen, jnp.exp(s - jnp.max(s, axis=-1, keepdims=True)), 0.0)
        p = (e / jnp.sum(e, axis=-1, keepdims=True)).astype(BF)
        att_ref[t] = jnp.dot(p, keys, preferred_element_type=F32).astype(BF)

    def from_a(zz):
        i = at(zz, 1 - a, b)
        for p in range(pa):
            got(i, p)
            ag(i, p, SIDE_B, peer_b).start()
        ag_core(i, c).start()

    if planar:
        from_a(z)

    def z_step(d, carry):
        pl.when(z - d >= 0)(lambda: share(z - d, True, go_up))
        pl.when(z + d < Z)(lambda: share(z + d, True, go_down))
        if planar:
            pl.when(z - d >= 0)(lambda: from_a(z - d))
            pl.when(z + d < Z)(lambda: from_a(z + d))
        return carry

    lax.fori_loop(1, Z, z_step, 0)

    if planar:
        def from_b(k, carry):
            attend(k)
            i = at((z + k // 2) % Z, k % 2, 1 - b)
            for p in range(pa):
                got(i, p)
            ag_core(i, c).start()
            return carry

        lax.fori_loop(0, 2 * Z, from_b, 0)
        first = min(2 * Z, R)
    else:
        first = 0
    for t in range(first, R):
        attend(t)

    pltpu.make_async_copy(att_ref, att_hbm, out_sem).start()

    def from_core(i, carry):
        ag_core(i, 1 - c).wait_recv()
        return carry

    lax.fori_loop(0, chips, from_core, 0)

    for src, dst, s in ((wg_hbm, wg, 0), (wu_hbm, wu, 1), (wd_hbm, wd, 2)):
        pltpu.make_async_copy(src.at[0], dst, w_sem.at[s]).wait()
    rows = n * R
    kc = 3584
    gacc[...] = jnp.zeros_like(gacc)
    uacc[...] = jnp.zeros_like(uacc)

    def k_step(k, carry):
        ks = pl.ds(pl.multiple_of(k * kc, kc), kc)
        xk = xs[:, :, :, ks].astype(F32).reshape(rows, kc).astype(BF)
        gacc[...] += jnp.dot(xk, wg[ks, :], preferred_element_type=F32)
        uacc[...] += jnp.dot(xk, wu[ks, :], preferred_element_type=F32)
        return carry

    lax.fori_loop(0, D // kc, k_step, 0)
    g = gacc[...]
    hidden = (g / (1.0 + jnp.exp(-g)) * uacc[...]).astype(BF)
    h3[...] = hidden.astype(F32).reshape(chips, 2, R, F)

    mine = place_ref[me].astype(F32)
    info = xs[:, :, :, pl.ds(D, EXTRA)].astype(F32).reshape(rows, EXTRA)
    levels = [info[:, top + k : top + k + 1] for k in range(top)]
    total = functools.reduce(lambda p, q: p + q, levels)
    coef = jnp.zeros((rows, 1), F32)
    for k in range(top):
        coef = coef + jnp.where(info[:, k : k + 1] == mine, route_scale * levels[k] / total, 0.0)
    cf[...] = jnp.broadcast_to(coef, (rows, EXTRA)).reshape(chips, 2, R, EXTRA)

    nc = 1792

    def down_half(cc):
        hh = h3[:, cc].reshape(chips * R, F).astype(BF)
        scale = cf[:, cc].reshape(chips * R, EXTRA)[:, :1]

        def n_step(k, carry):
            ns = pl.ds(pl.multiple_of(k * nc, nc), nc)
            p = jnp.dot(hh, wd[:, ns], preferred_element_type=F32).astype(BF).astype(F32)
            acc[:, cc, :, ns] = (p * scale).reshape(chips, R, nc).astype(BF)
            return carry

        lax.fori_loop(0, D // nc, n_step, 0)

    pr = rz_s.shape[1]
    wr = D // pr

    def cols(p):
        return pl.ds(p * wr, wr)

    def to_core(i):
        return pltpu.make_async_remote_copy(
            acc.at[i, 1 - c], rc.at[i], rsc_ss.at[i], rc_s.at[i], device_id={"expert": peer_c}
        )

    def to_b(zz, aa, p):
        i = at(zz, aa, 1 - b)
        return pltpu.make_async_remote_copy(
            acc.at[i, c, :, cols(p)], rb.at[zz, aa, :, cols(p)], rs_ss.at[SIDE_B, i, p],
            rb_s.at[zz, aa, p], device_id={"expert": peer_b},
        )

    def to_a(zz, p):
        i = at(zz, 1 - a, b)
        return pltpu.make_async_remote_copy(
            acc.at[i, c, :, cols(p)], ra.at[zz, :, cols(p)], rs_ss.at[SIDE_A, i, p],
            ra_s.at[zz, p], device_id={"expert": peer_a},
        )

    def to_z(zz, p):
        return pltpu.make_async_remote_copy(
            acc.at[at(zz, a, b), c, :, cols(p)], rz.at[z, :, cols(p)], rsz_ss.at[zz, p],
            rz_s.at[z, p], device_id={"expert": column_dev(zz)},
        )

    def from_z(zz, p):
        return pltpu.make_async_remote_copy(
            acc.at[chip, c, :, cols(p)], rz.at[zz, :, cols(p)], rsz_ss.at[zz, p],
            rz_s.at[zz, p], device_id={"expert": column_dev(zz)},
        )

    down_half(1 - c)

    def far(k):
        return (z + 1 + k) % Z

    def core_send(k, carry):
        if planar:
            q = k % (chips // 2)
            zz, other = far(q // 2), 1 - q % 2
            away = 1 - k // (chips // 2)
            aa = (1 - 2 * a) * away + a
            bb = (1 - 2 * b) * other + b
            to_core(at(zz, aa, bb)).start()
        else:
            to_core(far(k)).start()
        return carry

    lax.fori_loop(0, chips, core_send, 0)
    down_half(c)

    def plus(*terms):
        return functools.reduce(lambda p, q: p + q, [t.astype(F32) for t in terms])

    if planar:
        def b_send(k, carry):
            zz = far(k // 2)
            aa = (1 - 2 * a) * (1 - k % 2) + a
            i = at(zz, aa, 1 - b)
            to_core(i).wait_recv()
            acc[i, c] = plus(acc[i, c], rc[i]).astype(BF)
            for p in range(pr):
                to_b(zz, aa, p).start()
            return carry

        lax.fori_loop(0, 2 * Z, b_send, 0)

        def a_send(k):
            zz = far(k)
            i = at(zz, 1 - a, b)
            to_core(i).wait_recv()
            for p in range(pr):
                to_b(zz, 1 - a, p).wait_recv()
                cp = cols(p)
                acc[i, c, :, cp] = plus(acc[i, c, :, cp], rc[i, :, cp], rb[zz, 1 - a, :, cp]).astype(BF)
                to_a(zz, p).start()

        a_send(0)

    def column_sum(zz, p):
        i = at(zz, a, b)
        cp = cols(p)
        if planar:
            to_b(zz, a, p).wait_recv()
            to_a(zz, p).wait_recv()
            return plus(acc[i, c, :, cp], rc[i, :, cp], rb[zz, a, :, cp], ra[zz, :, cp])
        return plus(acc[i, c, :, cp], rc[i, :, cp])

    def z_send(k, carry):
        if planar:
            a_send(k + 1)
        zz = far(k)
        to_core(at(zz, a, b)).wait_recv()
        for p in range(pr):
            acc[at(zz, a, b), c, :, cols(p)] = column_sum(zz, p).astype(BF)
            to_z(zz, p).start()
        return carry

    lax.fori_loop(0, Z - 1, z_send, 0)
    to_core(chip).wait_recv()
    for p in range(pr):
        result = column_sum(z, p)
        for d in range(1, Z):
            zz = (z + d) % Z
            from_z(zz, p).wait_recv()
            result = result + rz[zz, :, cols(p)].astype(F32)
        moe_ref[:, cols(p)] = result.astype(BF)

    pltpu.make_async_copy(att_ref, att_hbm, out_sem).wait()

    def core_done(i, carry):
        ag_core(i, c).wait_send()
        to_core(i).wait_send()
        return carry

    lax.fori_loop(0, chips, core_done, 0)

    def z_done(zz, carry):
        i = at(zz, a, b)

        @pl.when(zz != z)
        def _():
            for p in range(pr):
                to_z(zz, p).wait_send()

        for p in range(pa):
            pl.when((zz <= z) & (z < Z - 1))(lambda: ag_z(zz, p, 0, me + 2 * plane).wait_send())
            pl.when((zz >= z) & (z > 0))(lambda: ag_z(zz, p, 1, me - 2 * plane).wait_send())
        if planar:
            for p in range(pa):
                ag(i, p, SIDE_A, peer_a).wait_send()
                for aa in range(2):
                    ag(at(zz, aa, b), p, SIDE_B, peer_b).wait_send()
            for p in range(pr):
                to_a(zz, p).wait_send()
                for aa in range(2):
                    to_b(zz, aa, p).wait_send()
        return carry

    lax.fori_loop(0, Z, z_done, 0)


def per_device(
    normed, expert_ids, gate_levels, placement, w_gate, w_up, w_down,
    q_latent, q_rope, cache_latent, cache_rope, lengths,
):
    n = lax.axis_size("expert")
    Z, Y, X = chip_grid(n)
    chips = n // 2
    R, D = normed.shape
    F = w_gate.shape[2]
    heads = q_latent.shape[1]
    vmem = pl.BlockSpec(memory_space=pltpu.VMEM)
    smem = pl.BlockSpec(memory_space=pltpu.SMEM)
    hbm = pl.BlockSpec(memory_space=pl.ANY)
    dma = pltpu.SemaphoreType.DMA
    side = Z if Y * X > 1 else 1
    pa, pr = parts(D + EXTRA, PA), parts(D, PR)
    return pl.pallas_call(
        functools.partial(body, n),
        out_shape=(
            jax.ShapeDtypeStruct((R, D), BF),
            jax.ShapeDtypeStruct(q_latent.shape, BF),
        ),
        in_specs=[vmem, vmem, vmem, smem, smem, hbm, hbm, hbm, hbm, vmem, hbm, hbm],
        out_specs=(vmem, hbm),
        scratch_shapes=[
            pltpu.VMEM((chips, 2, R, D + EXTRA), BF),
            pltpu.VMEM((chips, 2, R, D), BF),
            pltpu.VMEM((chips, R, D), BF),
            pltpu.VMEM((side, 2, R, D), BF),
            pltpu.VMEM((side, R, D), BF),
            pltpu.VMEM((Z, R, D), BF),
            pltpu.VMEM((D, F), BF),
            pltpu.VMEM((D, F), BF),
            pltpu.VMEM((F, D), BF),
            pltpu.VMEM((chips, 2, R, F), F32),
            pltpu.VMEM((chips, 2, R, EXTRA), F32),
            pltpu.VMEM((heads * R, 128), F32),
            pltpu.VMEM((n * R, F), F32),
            pltpu.VMEM((n * R, F), F32),
            pltpu.VMEM(q_latent.shape, BF),
            pltpu.VMEM(cache_latent.shape, BF),
            pltpu.VMEM(cache_rope.shape, BF),
            pltpu.VMEM(q_latent.shape, BF),
            dma((3,)),
            dma((3,)),
            dma,
            dma((2, chips, pa)),
            dma((chips, pa)),
            dma((2, Z, pa)),
            dma((chips,)),
            dma((chips,)),
            dma((2, chips, pr)),
            dma((Z, pr)),
            dma((chips,)),
            dma((chips,)),
            dma((side, 2, pr)),
            dma((side, pr)),
            dma((Z, pr)),
        ],
        compiler_params=pltpu.CompilerParams(
            collective_id=0, has_side_effects=True, vmem_limit_bytes=60 << 20
        ),
        cost_estimate=pl.CostEstimate(flops=3 * 10**9, bytes_accessed=13 * 10**6, transcendentals=300000),
    )(
        normed, expert_ids.T, gate_levels.T, lengths, placement, w_gate, w_up, w_down,
        q_latent, q_rope, cache_latent, cache_rope,
    )


def solution(mesh):
    rows = ("groups", "expert")
    in_specs = (
        P(rows, None), P(rows, None), P(rows, None), P(),
        P("expert", None, None), P("expert", None, None), P("expert", None, None),
        P(rows, None, None), P(rows, None), P(rows, None, None), P(rows, None, None), P(rows),
    )
    out_specs = (P(rows, None), P(rows, None, None))
    return jax.shard_map(
        per_device, mesh=mesh, in_specs=in_specs, out_specs=out_specs, check_vma=False
    )
```
